32 devices in a mesh: group: 2 (over x), seq: 8 (over z, y), res: 2 (over core).
Axes of the slice: x: 2, y: 2, z: 4, core: 2. Of those that a mesh axis runs over, the one named last changes fastest.
Arguments:
- alignment: bfloat16 [1024, 128, 256], P(('group', 'seq'), 'res'), parts along dimension 0, may hold values from -8 to 8
- ln_gain: float32 [256], replicated, may hold values from 0.5 to 1.5
- ln_bias: float32 [256], replicated, may hold values from -0.6 to 0.6
- w_left: bfloat16 [256, 32], replicated, may hold values from -0.375 to 0.375
- bias_left: float32 [32], replicated, may hold values from -0.6 to 0.6
- w_right: bfloat16 [256, 32], replicated, may hold values from -0.375 to 0.375
- bias_right: float32 [32], replicated, may hold values from -0.6 to 0.6
- w_out: bfloat16 [1024, 128], replicated, may hold values from -1.5 to 1.5
- bias_out: float32 [128], replicated, may hold values from -0.5 to 0.5
Outputs:
- pair_update: bfloat16 [256, 128, 128], P(('group', 'seq'), 'res'), parts along dimension 0
The draws below stay inside these ranges and needn't reach their ends.
There are 2 independent parts, one for each index of `group`. The reference program is written for one: setup_inputs(seed, part) draws one part's arguments, and reference() takes and returns one part's arrays. A program takes and returns all parts, laid end to end along the dimension named above; an argument that names none is the same for every part. Nothing has to cross between parts.
All inputs are finite; a program needn't handle non-finite values.
Results may differ from the reference program's by a relative error of at most 0.0034.
Values may be sent and summed in bfloat16 or wider, within the bound.
No kernel may reach another device: no remote copies, remote signals or barrier semaphores. Data moves between devices by JAX's collectives and lax.ppermute only.
A program may use at most 64 MiB of HBM per device.

```python
import math
import jax
import jax.numpy as jnp
from jax import lax

C = 256
PROJ = 32
OUT = 128
S_DEV = 64
S = 512
L = 128
N_SEQ = 8


def draw_alignment(key, part):
    factor_count = 16
    subkeys = jax.random.split(jax.random.fold_in(key, 11), 3)
    jitter = jax.random.normal(subkeys[0], (S, L, C), jnp.float32)
    loadings = jax.random.normal(subkeys[1], (S, factor_count), jnp.float32)
    shapes = jax.random.normal(subkeys[2], (factor_count, L * C), jnp.float32) / math.sqrt(factor_count)
    shared = jnp.dot(loadings, shapes, precision=lax.Precision.HIGHEST).reshape(S, L, C)
    return jnp.clip(jitter + shared, -8.0, 8.0).astype(jnp.bfloat16)


def gaussian(key, extent, scale, most, dtype=jnp.bfloat16):
    result = jax.random.normal(key, extent, jnp.float32) * scale
    return jnp.minimum(jnp.maximum(result, -most), most).astype(dtype)


def setup_inputs(seed: int = 0, part: int = 0) -> dict:
    keys = jax.random.split(jax.random.key(seed), 10)
    part_splits = jax.random.split(jax.random.fold_in(keys[9], part), 10)
    alignment = draw_alignment(jax.random.fold_in(jax.random.fold_in(keys[9], part), 71), part)
    ln_gain = jnp.clip(jax.random.uniform(keys[1], (C,), jnp.float32, 0.5, 1.5), 0.5, 1.5)
    ln_bias = gaussian(keys[2], (C,), 0.15, 0.6, jnp.float32)
    w_left = gaussian(keys[3], (C, PROJ), C ** -0.5, 0.375)
    bias_left = gaussian(keys[4], (PROJ,), 0.15, 0.6, jnp.float32)
    w_right = gaussian(keys[5], (C, PROJ), C ** -0.5, 0.375)
    bias_right = gaussian(keys[6], (PROJ,), 0.15, 0.6, jnp.float32)
    w_out = gaussian(keys[7], (PROJ * PROJ, OUT), (max(1, PROJ * PROJ // 64)) ** -0.5, 1.5)
    bias_out = jnp.clip(jax.random.uniform(keys[8], (OUT,), jnp.float32, -0.5, 0.5), -0.5, 0.5)
    return dict(alignment=alignment, ln_gain=ln_gain, ln_bias=ln_bias, w_left=w_left, bias_left=bias_left, w_right=w_right, bias_right=bias_right, w_out=w_out, bias_out=bias_out)


def normalize(alignment, ln_gain, ln_bias):
    values = alignment.astype(jnp.float32)
    center = lax.optimization_barrier(jnp.mean(values, axis=-1, keepdims=True))
    spread = lax.optimization_barrier(jnp.mean(jnp.square(values - center), axis=-1, keepdims=True))
    return ((values - center) * lax.rsqrt(spread + 1e-05) * ln_gain + ln_bias).astype(jnp.bfloat16)

def project(normed, weight, offset):
    flattened = normed.reshape(-1, normed.shape[-1])
    return (jnp.dot(flattened, weight, preferred_element_type=jnp.float32) + offset).astype(jnp.bfloat16)

def reference(alignment, ln_gain, ln_bias, w_left, bias_left, w_right, bias_right, w_out, bias_out):
    normed = normalize(alignment, ln_gain, ln_bias)
    left_groups = project(normed, w_left, bias_left).reshape(N_SEQ, S_DEV, L, PROJ)
    right_groups = project(normed, w_right, bias_right).reshape(N_SEQ, S_DEV, L, PROJ)
    weight_cube = w_out.astype(jnp.float32).reshape(PROJ, PROJ, OUT)
    height = math.gcd(L, 32)

    def group_step(summed, operands):
        left_group, right_group = operands
        right_wide = right_group.astype(jnp.float32)
        left_blocks = left_group.reshape(S_DEV, L // height, height, PROJ).transpose(1, 0, 2, 3)

        def block_term(left_block):
            outers = jnp.einsum('sic,sje->icej', left_block.astype(jnp.float32), right_wide)
            outers = lax.optimization_barrier(outers.astype(jnp.bfloat16)).astype(jnp.float32)
            return jnp.einsum('icej,ceo->ijo', outers, weight_cube)
        pieces = lax.map(block_term, left_blocks).reshape(L, L, OUT)
        return (summed + pieces, None)
    summed, unused = lax.scan(group_step, jnp.zeros((L, L, OUT), jnp.float32), (left_groups, right_groups))
    return (summed / S + bias_out).astype(jnp.bfloat16)
```

```python
import functools

import jax
import jax.numpy as jnp
from jax import lax
from jax.experimental import pallas as pl
from jax.experimental.pallas import tpu as pltpu
from jax.sharding import PartitionSpec as P

LANES = 128
ROWS = 16


def ring_order(count):
    return list(range(0, count, 2)) + [q for q in range(count - 1, -1, -1) if q % 2]


def project_kernel(
    x_ref, gain_ref, bias_ref, wl_ref, wr_ref, bl_ref, br_ref,
    left_ref, right_ref, values, normed, weights,
):
    seqs, residues, channels = x_ref.shape
    width = wl_ref.shape[0]
    fold = LANES // width
    groups = residues // fold

    @pl.when(pl.program_id(0) == 0)
    def _():
        row = lax.broadcasted_iota(jnp.int32, (width, LANES), 0)
        lane = lax.broadcasted_iota(jnp.int32, (width, LANES), 1)
        spread = (lane % width == row).astype(jnp.bfloat16)
        lane_wide = lax.broadcasted_iota(jnp.int32, (channels, LANES), 1)
        for side, w_ref in enumerate((wl_ref, wr_ref)):
            tiled = lax.dot_general(
                w_ref[...], spread, (((0,), (0,)), ((), ())), preferred_element_type=jnp.float32
            )
            for k in range(fold):
                weights[k * channels : (k + 1) * channels, side * LANES : (side + 1) * LANES] = (
                    jnp.where(lane_wide // width == k, tiled, 0.0).astype(jnp.bfloat16)
                )

    parts = channels // LANES
    for p in range(parts):
        values[p] = x_ref[:, :, p * LANES : (p + 1) * LANES].astype(jnp.float32).reshape(
            seqs * residues, LANES
        )
    gain = gain_ref[...]
    bias = bias_ref[...]

    for g in range(groups):
        for k in range(fold):
            v = jnp.concatenate(
                [values[p, pl.ds(g * fold + k, seqs, stride=residues), :] for p in range(parts)],
                axis=1,
            )
            center = jnp.mean(v, axis=-1, keepdims=True)
            d = v - center
            spread2 = jnp.mean(d * d, axis=-1, keepdims=True)
            normed[g * seqs : (g + 1) * seqs, k * channels : (k + 1) * channels] = (
                d * lax.rsqrt(spread2 + 1e-05) * gain + bias
            ).astype(jnp.bfloat16)
    offset = jnp.concatenate([bl_ref[...]] * fold + [br_ref[...]] * fold, axis=1)
    out = (
        jnp.dot(normed[...], weights[...], preferred_element_type=jnp.float32) + offset
    ).astype(jnp.bfloat16)
    for g in range(groups):
        rows = out[g * seqs : (g + 1) * seqs]
        left_ref[:, g * LANES : (g + 1) * LANES] = rows[:, :LANES]
        right_ref[:, g * LANES : (g + 1) * LANES] = rows[:, LANES:]


def project(alignment, ln_gain, ln_bias, w_left, bias_left, w_right, bias_right):
    seqs, residues, channels = alignment.shape
    width = w_left.shape[1]
    block = ROWS
    whole = lambda shape: pl.BlockSpec(shape, lambda s: (0,) * len(shape))
    wide = residues * width
    fold = LANES // width
    return pl.pallas_call(
        project_kernel,
        grid=(seqs // block,),
        in_specs=[
            pl.BlockSpec((block, residues, channels), lambda s: (s, 0, 0)),
            whole((1, channels)), whole((1, channels)),
            whole((width, channels)), whole((width, channels)),
            whole((1, width)), whole((1, width)),
        ],
        out_specs=[
            pl.BlockSpec((block, wide), lambda s: (s, 0)),
            pl.BlockSpec((block, wide), lambda s: (s, 0)),
        ],
        out_shape=[jax.ShapeDtypeStruct((seqs, wide), jnp.bfloat16)] * 2,
        scratch_shapes=[
            pltpu.VMEM((channels // LANES, block * residues, LANES), jnp.float32),
            pltpu.VMEM((block * residues // fold, fold * channels), jnp.bfloat16),
            pltpu.VMEM((fold * channels, 2 * LANES), jnp.bfloat16),
        ],
        name="project",
    )(
        alignment, ln_gain[None], ln_bias[None], w_left.T, w_right.T,
        bias_left[None], bias_right[None],
    )


def spread_weights(w_out, width):
    fold = LANES // width
    out_width = w_out.shape[1]
    cube = w_out.reshape(width, 1, width, 1, out_width)
    same = jnp.eye(fold, dtype=jnp.bool_)[None, :, None, :, None]
    return jnp.where(same, cube, jnp.zeros((), w_out.dtype)).reshape(
        width * fold * width, fold * out_width
    )


def pair_kernel(count, kept, width, scale, order_ref, left_ref, spread_ref, bias_ref, *refs):
    rights = refs[: count + 1]
    out_ref, lefts, turned, product, result = refs[count + 1 :]
    halves, _, half_rows, left_wide = left_ref.shape
    seqs = halves * half_rows
    wide = rights[0].shape[1]
    fold = LANES // width
    groups = wide // LANES
    out_width = spread_ref.shape[1] // fold
    for d in range(count):
        for h in range(halves):
            start = d * seqs + h * half_rows
            lefts[start : start + half_rows, :] = left_ref[h, order_ref[d]]
    row = lax.broadcasted_iota(jnp.int32, (width * ROWS, left_wide), 0)
    lane = lax.broadcasted_iota(jnp.int32, (width * ROWS, left_wide), 1)
    pick = (lane == (row % ROWS) * width + row // ROWS).astype(jnp.bfloat16)
    turned[...] = lax.dot_general(
        pick, lefts[...], (((1,), (1,)), ((), ())), preferred_element_type=jnp.float32
    ).astype(jnp.bfloat16)
    for g in range(0, groups, 2):
        many = min(2, groups - g)
        columns = jnp.concatenate(
            [r[:, g * LANES : (g + many) * LANES] for r in rights], axis=0
        )
        outer = jnp.dot(turned[...], columns, preferred_element_type=jnp.float32).astype(
            jnp.bfloat16
        )
        for m in range(many):
            for c in range(width):
                product[(g + m) * ROWS : (g + m + 1) * ROWS, c * LANES : (c + 1) * LANES] = outer[
                    c * ROWS : (c + 1) * ROWS, m * LANES : (m + 1) * LANES
                ]
    summed = jnp.dot(product[...], spread_ref[...], preferred_element_type=jnp.float32)
    columns_here = groups * fold
    for g in range(groups):
        for k in range(fold):
            result[pl.ds(g * fold + k, ROWS, stride=columns_here), :] = summed[
                g * ROWS : (g + 1) * ROWS, k * out_width : (k + 1) * out_width
            ]
    for i in range(kept):
        out_ref[i] = (
            result[i * columns_here : (i + 1) * columns_here, :] * scale + bias_ref[...]
        ).astype(jnp.bfloat16)


def pair_update(order, left, spread, bias_out, rights, kept, width, total):
    count = left.shape[1]
    wide = rights[0].shape[1]
    out_width = bias_out.shape[0]
    columns_here = wide // width
    vmem = pl.BlockSpec(memory_space=pltpu.VMEM)
    groups = wide // LANES
    return pl.pallas_call(
        functools.partial(pair_kernel, count, kept, width, 1.0 / total),
        in_specs=[pl.BlockSpec(memory_space=pltpu.SMEM)] + [vmem] * (3 + len(rights)),
        out_specs=vmem,
        out_shape=jax.ShapeDtypeStruct((kept, columns_here, out_width), jnp.bfloat16),
        scratch_shapes=[
            pltpu.VMEM((total, left.shape[3]), jnp.bfloat16),
            pltpu.VMEM((width * ROWS, total), jnp.bfloat16),
            pltpu.VMEM((groups * ROWS, width * LANES), jnp.bfloat16),
            pltpu.VMEM((ROWS * columns_here, out_width), jnp.float32),
        ],
        name="pair",
    )(order, left, spread, bias_out[None], *rights)


def shards(alignment, ln_gain, ln_bias, w_left, bias_left, w_right, bias_right, w_out, bias_out):
    seqs, residues, _ = alignment.shape
    width = w_left.shape[1]
    count = lax.axis_size("seq")
    pair = lax.axis_size("res")
    kept = residues * pair // count
    left, right = project(alignment, ln_gain, ln_bias, w_left, bias_left, w_right, bias_right)
    spread = spread_weights(w_out, width)

    order = ring_order(count)
    ahead = [(order[p], order[(p + 1) % count]) for p in range(count)]
    back = [(b, a) for a, b in ahead]
    place = [order.index(q) for q in range(count)]
    position = jnp.asarray(place, jnp.int32)[lax.axis_index("seq")]

    rights = [right]
    offsets = [0]
    up = down = right
    for d in range(1, count // 2):
        up = lax.ppermute(up, "seq", ahead)
        down = lax.ppermute(down, "seq", back)
        rights += [up, down]
        offsets += [-d, d]
    half = seqs // 2
    rights += [
        lax.ppermute(up[:half], "seq", ahead), lax.ppermute(down[half:], "seq", back)
    ]
    offsets += [count // 2]
    sources = jnp.asarray(order, jnp.int32)[(position + jnp.asarray(offsets, jnp.int32)) % count]

    blocks = left.reshape(pair, seqs // pair, count // pair, kept * width).transpose(0, 2, 1, 3)
    blocks = lax.all_to_all(blocks, "res", 0, 0, tiled=True)
    blocks = blocks.reshape(count, seqs // pair, kept * width)
    blocks = lax.all_to_all(blocks, "seq", 0, 0, tiled=True)
    blocks = lax.all_gather(blocks, "res", axis=0)
    return pair_update(
        sources, blocks, spread, bias_out, rights, kept, width, seqs * count
    )


def solution(mesh):
    return jax.shard_map(
        shards,
        mesh=mesh,
        in_specs=(P(("group", "seq"), "res", None), P(), P(), P(), P(), P(), P(), P(), P()),
        out_specs=P(("group", "seq"), "res", None),
        check_vma=False,
    )
```

```python
import functools

import jax
import jax.numpy as jnp
from jax import lax
from jax.experimental import pallas as pl
from jax.experimental.pallas import tpu as pltpu
from jax.sharding import PartitionSpec as P


LANES = 128
ROWS = 16
TILE = 8
STREAMS = 2


def ring_order(count):
    return list(range(0, count, 2)) + [q for q in range(count - 1, -1, -1) if q % 2]


def ring_source(count, offset):
    me = lax.axis_index("seq")
    place = jnp.where(me % 2 == 0, me // 2, count - 1 - me // 2)
    there = lax.rem(place + offset + count, count)
    return jnp.where(there < count // 2, 2 * there, 2 * (count - 1 - there) + 1)


def project_kernel(
    x_ref, gain_ref, bias_ref, wl_ref, wr_ref, bl_ref, br_ref, *refs
):
    rights, (kept_ref, sent_ref, values, normed, weights, offset) = refs[:-6], refs[-6:]
    seqs, residues, channels = x_ref.shape
    width = wl_ref.shape[0]
    fold = LANES // width
    groups = residues // fold
    parts = channels // LANES
    step = pl.program_id(0)

    @pl.when(step == 0)
    def _():
        row = lax.broadcasted_iota(jnp.int32, (width, LANES), 0)
        lane = lax.broadcasted_iota(jnp.int32, (width, LANES), 1)
        spread = (lane % width == row).astype(jnp.bfloat16)
        lane_wide = lax.broadcasted_iota(jnp.int32, (channels, LANES), 1)
        for side, (w_ref, b_ref) in enumerate(((wl_ref, bl_ref), (wr_ref, br_ref))):
            tiled = lax.dot_general(
                w_ref[...], spread, (((0,), (0,)), ((), ())), preferred_element_type=jnp.float32
            )
            here = slice(side * LANES, (side + 1) * LANES)
            for k in range(fold):
                weights[k * channels : (k + 1) * channels, here] = (
                    jnp.where(lane_wide // width == k, tiled, 0.0).astype(jnp.bfloat16)
                )
            offset[:, here] = jnp.concatenate([b_ref[...]] * fold, axis=1)

    for p in range(parts):
        for t in range(residues // TILE):
            values[p, t * seqs * TILE : (t + 1) * seqs * TILE, :] = (
                x_ref[:, t * TILE : (t + 1) * TILE, p * LANES : (p + 1) * LANES]
                .astype(jnp.float32)
                .reshape(seqs * TILE, LANES)
            )
    gain = gain_ref[...]
    bias = bias_ref[...]
    for g in range(groups):
        for k in range(fold):
            residue = g * fold + k
            at = residue // TILE * seqs * TILE + residue % TILE
            v = [values[p, pl.ds(at, seqs, stride=TILE), :] for p in range(parts)]
            center = jnp.sum(sum(v), axis=-1, keepdims=True) * (1.0 / channels)
            d = [u - center for u in v]
            spread = jnp.sum(sum(u * u for u in d), axis=-1, keepdims=True) * (1.0 / channels)
            scale = lax.rsqrt(spread + 1e-05)
            for p in range(parts):
                here = slice(p * LANES, (p + 1) * LANES)
                at = k * channels + p * LANES
                normed[g * seqs : (g + 1) * seqs, at : at + LANES] = (
                    d[p] * scale * gain[:, here] + bias[:, here]
                ).astype(jnp.bfloat16)
    out = (
        jnp.dot(normed[...], weights[...], preferred_element_type=jnp.float32) + offset[...]
    ).astype(jnp.bfloat16)
    each = groups // len(rights)
    for g in range(groups):
        at = (g % each) * LANES
        rights[g // each][:, at : at + LANES] = out[g * seqs : (g + 1) * seqs, LANES:]
    _, half_rows, wide = kept_ref.shape
    rows_here = pl.ds(pl.multiple_of(lax.rem(step * seqs, half_rows), seqs), seqs)

    def store_left(ref):
        for g in range(groups):
            at = g * LANES
            ref[at // wide, rows_here, at % wide : at % wide + LANES] = out[
                g * seqs : (g + 1) * seqs, :LANES
            ]

    mine = step * seqs // half_rows == lax.axis_index("res")
    pl.when(mine)(lambda: store_left(kept_ref))
    pl.when(jnp.logical_not(mine))(lambda: store_left(sent_ref))


def in_hbm(value):
    return pltpu.with_memory_space_constraint(value, pltpu.HBM)


def project(streams, count, pair, alignment, vectors, weights):
    seqs, residues, channels = alignment.shape
    ln_gain, ln_bias, bias_left, bias_right = vectors
    w_left, w_right = weights
    width = w_left.shape[1]
    fold = LANES // width
    block = ROWS
    low = count // pair
    wide = residues * width // streams
    left_shape = (low, seqs // pair, residues * width // low)
    whole = lambda shape: pl.BlockSpec(shape, lambda s: (0,) * len(shape))
    return pl.pallas_call(
        project_kernel,
        grid=(seqs // block,),
        in_specs=[
            pl.BlockSpec((block, residues, channels), lambda s: (s, 0, 0)),
            whole((1, channels)), whole((1, channels)),
            whole((width, channels)), whole((width, channels)),
            whole((1, width)), whole((1, width)),
        ],
        out_specs=[pl.BlockSpec((block, wide), lambda s: (s, 0))] * streams
        + [whole(left_shape)] * 2,
        out_shape=[jax.ShapeDtypeStruct((seqs, wide), jnp.bfloat16)] * streams
        + [jax.ShapeDtypeStruct(left_shape, jnp.bfloat16)] * 2,
        scratch_shapes=[
            pltpu.VMEM((channels // LANES, block * residues, LANES), jnp.float32),
            pltpu.VMEM((block * residues // fold, fold * channels), jnp.bfloat16),
            pltpu.VMEM((fold * channels, 2 * LANES), jnp.bfloat16),
            pltpu.VMEM((1, 2 * LANES), jnp.float32),
        ],
        compiler_params=pltpu.CompilerParams(vmem_limit_bytes=16 << 20),
        name="project",
    )(
        in_hbm(alignment), in_hbm(ln_gain[None]), in_hbm(ln_bias[None]), in_hbm(w_left.T),
        in_hbm(w_right.T), in_hbm(bias_left[None]), in_hbm(bias_right[None]),
    )


def pack_kernel(count, reach, kept_ref, got_ref, right_ref, up_ref, down_ref, far_ref, own_ref):
    low, half_rows, wide = kept_ref.shape
    seqs = right_ref.shape[0]
    core = lax.axis_index("res")
    up_ref[:seqs] = right_ref[...]
    down_ref[:seqs] = right_ref[...]
    offsets = [0, count // 2] + [sign * d for d in range(1, reach + 1) for sign in (1, -1)]
    for offset in offsets:
        there = ring_source(count, offset)
        held = there // low == core
        block = lax.rem(there, low)

        def put(ref):
            if offset == 0:
                own_ref[...] = ref[block]
            elif offset == count // 2:
                far_ref[...] = ref[block]
            else:
                to = up_ref if offset > 0 else down_ref
                at = seqs + (reach - abs(offset)) * (half_rows // 2)
                to[at : at + half_rows // 2, :wide] = ref[block, : half_rows // 2]
                to[at : at + half_rows // 2, wide : 2 * wide] = ref[block, half_rows // 2 :]

        pl.when(held)(functools.partial(put, kept_ref))
        pl.when(jnp.logical_not(held))(functools.partial(put, got_ref))


def pack(count, reach, kept, got, right):
    _, half_rows, wide = kept.shape
    seqs, right_wide = right.shape
    vmem = pl.BlockSpec(memory_space=pltpu.VMEM)
    message = jax.ShapeDtypeStruct((seqs + reach * half_rows // 2, right_wide), jnp.bfloat16)
    piece = jax.ShapeDtypeStruct((half_rows, wide), jnp.bfloat16)
    return pl.pallas_call(
        functools.partial(pack_kernel, count, reach),
        in_specs=[vmem] * 3,
        out_specs=[vmem] * 4,
        out_shape=[message, message, piece, piece],
        compiler_params=pltpu.CompilerParams(vmem_limit_bytes=8 << 20),
        name="pack",
    )(kept, got, right)


def line_kernel(own_ref, far_ref, *refs):
    messages, out_ref = refs[:-1], refs[-1]
    count, half_rows, wide = out_ref.shape
    out_ref[0] = own_ref[...]
    for d, ref in enumerate(messages):
        at = ref.shape[0] - half_rows // 2
        out_ref[1 + d, : half_rows // 2] = ref[at:, :wide]
        out_ref[1 + d, half_rows // 2 :] = ref[at:, wide : 2 * wide]
    out_ref[count - 1] = far_ref[...]


def line(count, own, far, messages):
    vmem = pl.BlockSpec(memory_space=pltpu.VMEM)
    return pl.pallas_call(
        line_kernel,
        in_specs=[vmem] * (2 + len(messages)),
        out_specs=vmem,
        out_shape=jax.ShapeDtypeStruct((count, *own.shape), jnp.bfloat16),
        compiler_params=pltpu.CompilerParams(vmem_limit_bytes=8 << 20),
        name="line",
    )(own, far, *messages)


def turn_kernel(width, mine_ref, other_ref, out_ref, lined):
    count, half_rows, wide = mine_ref.shape
    core = lax.axis_index("res")
    for r, halves in enumerate(((mine_ref, other_ref), (other_ref, mine_ref))):

        @pl.when(core == r)
        def _():
            for d in range(count):
                for h, ref in enumerate(halves):
                    at = (2 * d + h) * half_rows
                    lined[at : at + half_rows, :] = ref[d]

    row = lax.broadcasted_iota(jnp.int32, (width * ROWS, wide), 0)
    lane = lax.broadcasted_iota(jnp.int32, (width * ROWS, wide), 1)
    pick = (lane == (row % ROWS) * width + row // ROWS).astype(jnp.bfloat16)
    out_ref[...] = lax.dot_general(
        pick, lined[...], (((1,), (1,)), ((), ())), preferred_element_type=jnp.float32
    ).astype(jnp.bfloat16)


def turn(width, mine, other):
    count, half_rows, wide = mine.shape
    vmem = pl.BlockSpec(memory_space=pltpu.VMEM)
    return pl.pallas_call(
        functools.partial(turn_kernel, width),
        in_specs=[vmem] * 2,
        out_specs=vmem,
        out_shape=jax.ShapeDtypeStruct((width * ROWS, count * 2 * half_rows), jnp.bfloat16),
        scratch_shapes=[pltpu.VMEM((count * 2 * half_rows, wide), jnp.bfloat16)],
        compiler_params=pltpu.CompilerParams(vmem_limit_bytes=16 << 20),
        name="turn",
    )(mine, other)


def pair_kernel(streams, kept, width, scale, turned, w_ref, bias_ref, *refs):
    rights, (out_ref, product, result, spread) = refs[:-4], refs[-4:]
    each = len(rights) // streams
    seqs, wide = rights[0].shape
    fold = LANES // width
    groups = wide // LANES
    out_width = w_ref.shape[1]
    spread[...] = jnp.zeros_like(spread)
    for c in range(width):
        for k in range(fold):
            at = (c * fold + k) * width
            spread[at : at + width, k * out_width : (k + 1) * out_width] = w_ref[
                c * width : (c + 1) * width, :
            ]
    for t in range(streams):
        for g in range(0, groups, 2):
            many = min(2, groups - g)
            columns = jnp.concatenate(
                [
                    r[: min(seqs, r.shape[0]), g * LANES : (g + many) * LANES]
                    for r in rights[t * each : (t + 1) * each]
                ],
                axis=0,
            )
            outer = jnp.dot(turned[...], columns, preferred_element_type=jnp.float32).astype(
                jnp.bfloat16
            )
            for m in range(many):
                at = (t * groups + g + m) * ROWS
                for c in range(width):
                    product[at : at + ROWS, c * LANES : (c + 1) * LANES] = outer[
                        c * ROWS : (c + 1) * ROWS, m * LANES : (m + 1) * LANES
                    ]
    summed = jnp.dot(product[...], spread[...], preferred_element_type=jnp.float32)
    columns_here = streams * groups * fold
    for g in range(streams * groups):
        for k in range(fold):
            column = summed[g * ROWS : (g + 1) * ROWS, k * out_width : (k + 1) * out_width]
            for h in range(0, ROWS, TILE):
                at = h * columns_here + (g * fold + k) * TILE
                result[at : at + TILE, :] = column[h : h + TILE]
    for i in range(kept):
        at = i // TILE * TILE * columns_here + i % TILE
        out_ref[i] = (
            result[pl.ds(at, columns_here, stride=TILE), :] * scale + bias_ref[...]
        ).astype(jnp.bfloat16)


def pair_update(turned, w_out, bias_out, streams, kept, width):
    total = turned.shape[1]
    wide = streams[0][0].shape[1] * len(streams)
    out_width = bias_out.shape[0]
    fold = LANES // width
    vmem = pl.BlockSpec(memory_space=pltpu.VMEM)
    rights = [r for stream in streams for r in stream]
    return pl.pallas_call(
        functools.partial(pair_kernel, len(streams), kept, width, 1.0 / total),
        in_specs=[vmem] * (3 + len(rights)),
        out_specs=vmem,
        out_shape=jax.ShapeDtypeStruct((kept, wide // width, out_width), jnp.bfloat16),
        scratch_shapes=[
            pltpu.VMEM((wide // LANES * ROWS, width * LANES), jnp.bfloat16),
            pltpu.VMEM((ROWS * wide // width, out_width), jnp.float32),
            pltpu.VMEM((width * LANES, fold * out_width), jnp.bfloat16),
        ],
        compiler_params=pltpu.CompilerParams(vmem_limit_bytes=32 << 20),
        name="pair",
    )(turned, w_out, bias_out[None], *rights)


def shards(alignment, ln_gain, ln_bias, w_left, bias_left, w_right, bias_right, w_out, bias_out):
    seqs, residues, _ = alignment.shape
    width = w_left.shape[1]
    count = lax.axis_size("seq")
    pair = lax.axis_size("res")
    kept = residues * pair // count
    vectors = (ln_gain, ln_bias, bias_left, bias_right)

    order = ring_order(count)
    ahead = [(order[p], order[(p + 1) % count]) for p in range(count)]
    back = [(b, a) for a, b in ahead]
    half = seqs // 2

    *rights, left_kept, left_sent = project(
        STREAMS, count, pair, alignment, vectors, (w_left, w_right)
    )

    def hop(value, pairs, axes="seq"):
        return lax.ppermute(value, axes, pairs)

    left_got = hop(left_sent, [(0, 1), (1, 0)], "res")
    reach = count // 2 - 1
    up_first, down_first, far, own = pack(count, reach, left_kept, left_got, rights[-1])
    across = [(order[p], order[(p + count // 2) % count]) for p in range(count)]
    far = hop(far, across)

    streams = [[right] for right in rights]
    for t in range(STREAMS):
        up = down = rights[t]
        if t == STREAMS - 1:
            up, down = up_first, down_first
        for d in range(1, count // 2 + 1):
            if d == count // 2:
                up, down = up[:half], down[half:seqs]
            elif t == STREAMS - 1:
                rows = seqs + (reach - d + 1) * (seqs // pair // 2)
                up, down = up[:rows], down[:rows]
            up = hop(up, ahead)
            down = hop(down, back)
            streams[t] += [up, down]

    mine = line(count, own, far, streams[-1][1 : 1 + 2 * reach])
    other = hop(mine, [(0, 1), (1, 0)], "res")
    turned = turn(width, mine, other)
    return pair_update(turned, w_out, bias_out, streams, kept, width)


def solution(mesh):
    return jax.shard_map(
        shards,
        mesh=mesh,
        in_specs=(P(("group", "seq"), "res", None), P(), P(), P(), P(), P(), P(), P(), P()),
        out_specs=P(("group", "seq"), "res", None),
        check_vma=False,
    )
```
